32 devices in a mesh: dp: 8 (over z, x), heads: 4 (over y, core).
Axes of the slice: x: 2, y: 2, z: 4, core: 2. Of those that a mesh axis runs over, the one named last changes fastest.
Arguments:
- byte_states: bfloat16 [4096, 1280], P('dp'), may hold values from -6 to 6
- patch_states: bfloat16 [1024, 4096], P('dp'), may hold values from -6 to 6
- patch_lengths: int32 [8, 128], P('dp'), may hold values from 1 to 16, 512 in all within a row
- cotangent: bfloat16 [4096, 1280], P('dp'), may hold values from -6 to 6
- attention_gain: float32 [1280], replicated, may hold values from 0.5 to 2
- feedforward_gain: float32 [1280], replicated, may hold values from 0.5 to 1.5
- query_weight: bfloat16 [1280, 1024], P(None, 'heads'), may hold values from -0.15625 to 0.15625
- key_weight: bfloat16 [4096, 1024], P(None, 'heads'), may hold values from -0.09375 to 0.09375
- value_weight: bfloat16 [4096, 1024], P(None, 'heads'), may hold values from -0.09375 to 0.09375
- output_weight: bfloat16 [1024, 1280], P('heads'), may hold values from -0.1875 to 0.1875
- gate_weight: bfloat16 [1280, 3584], P(None, 'heads'), may hold values from -0.15625 to 0.15625
- up_weight: bfloat16 [1280, 3584], P(None, 'heads'), may hold values from -0.15625 to 0.15625
- down_weight: bfloat16 [3584, 1280], P('heads'), may hold values from -0.09375 to 0.09375
- adam_first: float32 [4, 6193152], P('heads', 'dp'), may hold values from -0.6 to 0.6
- adam_second: float32 [4, 6193152], P('heads', 'dp'), may hold values from 0.001 to 0.1
Outputs:
- input_grad: bfloat16 [4096, 1280], P(('dp', 'heads'))
- patch_grad: bfloat16 [1024, 4096], P(('dp', 'heads'))
- new_first: float32 [4, 6193152], P('heads', 'dp')
- new_second: float32 [4, 6193152], P('heads', 'dp')
- adam_step: float32 [4, 6193152], P('heads', 'dp')
The draws below stay inside these ranges and needn't reach their ends.
Inputs may be any that keep to these rules, and one draw needn't show every extreme that they name: `patch_lengths`: row s holds the lengths in bytes of the 128 patches of sequence s in order; each row sums to 512.
All inputs are finite; a program needn't handle non-finite values.
Results may differ from the reference program's by a relative error of at most 0.039.
Values may be sent and summed in bfloat16 or wider, within the bound.
No kernel may reach another device: no remote copies, remote signals or barrier semaphores. Data moves between devices by JAX's collectives and lax.ppermute only.
A program may use at most 128 MiB of HBM per device.

```python
import math
import jax
import jax.numpy as jnp
import numpy as np
from jax import lax

D = 1280
DG = 4096
HEADS = 8
HEAD = 128
FF = 3584
BYTES = 512
MOST = 16
PATCHES = 128
GROUPS = 4
SEQS = 8
TOKENS = 4096
NPATCH = 1024
PER = 6193152
N_DP = 8


def shard_levels(key, dims, split, low, largest):
    loudness = 1.0
    for axis_at, blocks in split:
        steps = jax.random.uniform(jax.random.fold_in(jax.random.fold_in(key, 6), axis_at), (blocks,), jnp.float32, low / len(split), largest / len(split))
        loudness = loudness * jnp.repeat(jnp.exp(steps), dims[axis_at] // blocks).reshape((-1,) + (1,) * (len(dims) - 1 - axis_at))
    return loudness


def length_profile(count, total, limit, lean):
    weights = [(1 << 20) // math.isqrt(standing ** lean) + 1 for standing in range(2, count + 1)]
    rest, holding = total - limit - (count - 1), [1] * (count - 1)
    while rest > 0:
        free = [i for i in range(count - 1) if holding[i] < limit]
        whole, remaining = sum([weights[i] for i in free]), rest
        for i in free:
            addition = min(limit - holding[i], max(1, remaining * weights[i] // whole), rest)
            holding[i] = holding[i] + addition
            rest = rest - addition
    return np.array([limit] + holding)


def ragged(stream_key, amount, total, most, skew):
    if amount == 2:
        one = jax.random.randint(stream_key, (), max(1, total - most), min(most, total - 1) + 1)
        return jnp.stack([one, total - one])
    sizes = jnp.asarray(length_profile(amount, total, most, skew), jnp.int32)
    pairs = (amount - 1) // 2
    source_of, taker = sizes[1:1 + 2 * pairs:2], sizes[2:2 + 2 * pairs:2]
    room = jnp.minimum(source_of - 1, most - taker)
    moved = jax.random.randint(jax.random.fold_in(stream_key, 1), (pairs,), 0, 1 << 20) % (room + 1)
    sizes = sizes.at[1:1 + 2 * pairs:2].set(source_of - moved).at[2:2 + 2 * pairs:2].set(taker + moved)
    return sizes[jax.random.permutation(jax.random.fold_in(stream_key, 2), amount)]


def scatter_about(stream_key, dims, spread, bound, cuts=(), held_as=jnp.bfloat16):
    gain = shard_levels(stream_key, dims, cuts, -0.22, 0.18) if cuts else 1.0
    values = jax.random.normal(stream_key, dims, jnp.float32) * spread * gain
    return jnp.minimum(jnp.maximum(values, -bound), bound).astype(held_as)


def setup_inputs(seed: int = 0) -> dict:
    seeds = jax.random.split(jax.random.key(seed), 16)
    byte_states = scatter_about(seeds[0], (TOKENS, D), 1.0, 6.0, ((0, 8),))
    patch_states = scatter_about(seeds[1], (NPATCH, DG), 1.0, 6.0, ((0, 8),))
    patch_lengths = jax.vmap(lambda own: ragged(own, PATCHES, BYTES, MOST, 2))(jax.random.split(seeds[2], SEQS)).reshape((SEQS, PATCHES)).astype(jnp.int32)
    cotangent = scatter_about(seeds[3], (TOKENS, D), 1.0, 6.0, ((0, 8),))
    attention_gain = jnp.clip(jnp.exp(jax.random.uniform(seeds[4], (D,), jnp.float32, math.log(0.5), math.log(2.0))), 0.5, 2.0)
    feedforward_gain = jnp.clip(1.0 + 0.1 * jax.random.normal(seeds[5], (D,), jnp.float32), 0.5, 1.5)
    query_weight = scatter_about(seeds[6], (D, HEADS * HEAD), D ** -0.5, 0.15625, ((1, 4),))
    key_weight = scatter_about(seeds[7], (DG, HEADS * HEAD), DG ** -0.5, 0.09375, ((1, 4),))
    value_weight = scatter_about(seeds[8], (DG, HEADS * HEAD), DG ** -0.5, 0.09375, ((1, 4),))
    output_weight = scatter_about(seeds[9], (HEADS * HEAD, D), (HEADS * HEAD) ** -0.5, 0.1875, ((0, 4),))
    gate_weight = scatter_about(seeds[10], (D, FF), D ** -0.5, 0.15625, ((1, 4),))
    up_weight = scatter_about(seeds[11], (D, FF), D ** -0.5, 0.15625, ((1, 4),))
    down_weight = scatter_about(seeds[12], (FF, D), FF ** -0.5, 0.09375, ((0, 4),))
    adam_first = scatter_about(seeds[13], (GROUPS, PER), 0.1, 0.6, ((0, 4), (1, 8)), jnp.float32)
    adam_second = jnp.clip(jnp.exp(math.log(0.1) - 4.6051702 * jax.random.uniform(seeds[14], (GROUPS, PER), jnp.float32) ** shard_levels(seeds[14], (GROUPS, PER), ((0, 4), (1, 8)), -0.2, 0.2)), 0.001, 0.1)
    return {"byte_states": byte_states, "patch_states": patch_states, "patch_lengths": patch_lengths, "cotangent": cotangent, "attention_gain": attention_gain, "feedforward_gain": feedforward_gain, "query_weight": query_weight, "key_weight": key_weight, "value_weight": value_weight, "output_weight": output_weight, "gate_weight": gate_weight, "up_weight": up_weight, "down_weight": down_weight, "adam_first": adam_first, "adam_second": adam_second}


norm_epsilon = 1e-05
adam_epsilon = 1e-08
beta_first = 0.9
beta_second = 0.95
score_scale = 0.125
bias_first = 1.0 - 0.9 ** 20
bias_second = 1.0 - 0.95 ** 20

def norm_forward(inputs, gain_vec):
    inverse = lax.rsqrt(lax.optimization_barrier(jnp.mean(inputs * inputs, axis=-1, keepdims=True)) + norm_epsilon)
    return inputs * inverse * gain_vec

def norm_backward(inputs, gain_vec, grad_vec):
    inverse = lax.rsqrt(lax.optimization_barrier(jnp.mean(inputs * inputs, axis=-1, keepdims=True)) + norm_epsilon)
    scaled = grad_vec * gain_vec
    inner = lax.optimization_barrier(jnp.mean(scaled * inputs, axis=-1, keepdims=True))
    return inverse * scaled - inputs * (inverse * inverse * inverse) * inner

def rounded(values_in):
    return lax.optimization_barrier(values_in.astype(jnp.bfloat16)).astype(jnp.float32)

def group_total(group_terms):
    running_sum = jnp.zeros(group_terms[0].shape, jnp.float32)
    for group_term in group_terms:
        running_sum = running_sum + rounded(group_term)
    return running_sum

def matmul_plain(left, right):
    return jnp.dot(left, right, preferred_element_type=jnp.float32)

def reference(byte_states, patch_states, patch_lengths, cotangent, attention_gain, feedforward_gain, query_weight, key_weight, value_weight, output_weight, gate_weight, up_weight, down_weight, adam_first, adam_second):
    head_cols = HEADS * HEAD // GROUPS
    unit_cols = FF // GROUPS
    byte_float = byte_states.astype(jnp.float32)
    normed_bytes = norm_forward(byte_float, attention_gain).astype(jnp.bfloat16)
    query_full = matmul_plain(normed_bytes, query_weight).reshape(TOKENS, HEADS, HEAD)
    key_full = matmul_plain(patch_states, key_weight).reshape(NPATCH, HEADS, HEAD)
    value_proj = matmul_plain(patch_states, value_weight).astype(jnp.bfloat16)
    query_normed = norm_forward(query_full, 1.0).astype(jnp.bfloat16)
    key_normed = norm_forward(key_full, 1.0).astype(jnp.bfloat16)
    query_seq = query_normed.reshape(SEQS, BYTES, HEADS, HEAD).astype(jnp.float32)
    key_seq = key_normed.reshape(SEQS, PATCHES, HEADS, HEAD).astype(jnp.float32)
    value_seq = value_proj.reshape(SEQS, PATCHES, HEADS, HEAD).astype(jnp.float32)
    starts = jnp.cumsum(patch_lengths, axis=1) - patch_lengths
    positions = jnp.arange(BYTES, dtype=jnp.int32)
    visible = (starts[:, None, :] <= positions[None, :, None]).astype(jnp.float32)[:, None]
    scores = score_scale * jnp.einsum('sbhd,sphd->shbp', query_seq, key_seq)
    weights = jnp.exp(scores) * visible
    probabilities = weights / lax.optimization_barrier(jnp.sum(weights, axis=-1, keepdims=True))
    prob_half = rounded(probabilities)
    attended = jnp.einsum('shbp,sphd->sbhd', prob_half, value_seq).astype(jnp.bfloat16).reshape(TOKENS, HEADS * HEAD)
    attention_sum = group_total([matmul_plain(attended[:, group * head_cols:(group + 1) * head_cols], output_weight[group * head_cols:(group + 1) * head_cols]) for group in range(GROUPS)])
    residual = byte_float + attention_sum
    normed_hidden = norm_forward(residual, feedforward_gain).astype(jnp.bfloat16)
    gate = matmul_plain(normed_hidden, gate_weight)
    up_vals = matmul_plain(normed_hidden, up_weight)
    sigmoid = jax.nn.sigmoid(gate)
    activated = gate * sigmoid
    hidden = (activated * up_vals).astype(jnp.bfloat16)
    hidden_grad = matmul_plain(cotangent, down_weight.T)
    gate_grad = (hidden_grad * up_vals * (sigmoid * (1.0 + gate * (1.0 - sigmoid)))).astype(jnp.bfloat16)
    up_grad = (hidden_grad * activated).astype(jnp.bfloat16)
    normed_hidden_grad = group_total([matmul_plain(gate_grad[:, group * unit_cols:(group + 1) * unit_cols], gate_weight[:, group * unit_cols:(group + 1) * unit_cols].T) + matmul_plain(up_grad[:, group * unit_cols:(group + 1) * unit_cols], up_weight[:, group * unit_cols:(group + 1) * unit_cols].T) for group in range(GROUPS)])
    residual_grad = cotangent.astype(jnp.float32) + norm_backward(residual, feedforward_gain, normed_hidden_grad)
    residual_half = residual_grad.astype(jnp.bfloat16)
    attended_grad = matmul_plain(residual_half, output_weight.T).astype(jnp.bfloat16)
    attended_seq = attended_grad.reshape(SEQS, BYTES, HEADS, HEAD).astype(jnp.float32)
    prob_grad = jnp.einsum('sbhd,sphd->shbp', attended_seq, value_seq)
    score_grad = rounded(score_scale * probabilities * (prob_grad - lax.optimization_barrier(jnp.sum(probabilities * prob_grad, axis=-1, keepdims=True))))
    query_normed_grad = jnp.einsum('shbp,sphd->sbhd', score_grad, key_seq).reshape(TOKENS, HEADS, HEAD)
    key_normed_grad = jnp.einsum('shbp,sbhd->sphd', score_grad, query_seq).reshape(NPATCH, HEADS, HEAD)
    value_grad = jnp.einsum('shbp,sbhd->sphd', prob_half, attended_seq).astype(jnp.bfloat16).reshape(NPATCH, HEADS * HEAD)
    query_grad = norm_backward(query_full, 1.0, query_normed_grad).astype(jnp.bfloat16).reshape(TOKENS, HEADS * HEAD)
    key_grad = norm_backward(key_full, 1.0, key_normed_grad).astype(jnp.bfloat16).reshape(NPATCH, HEADS * HEAD)
    normed_bytes_grad = group_total([matmul_plain(query_grad[:, group * head_cols:(group + 1) * head_cols], query_weight[:, group * head_cols:(group + 1) * head_cols].T) for group in range(GROUPS)])
    patch_total = group_total([matmul_plain(key_grad[:, group * head_cols:(group + 1) * head_cols], key_weight[:, group * head_cols:(group + 1) * head_cols].T) + matmul_plain(value_grad[:, group * head_cols:(group + 1) * head_cols], value_weight[:, group * head_cols:(group + 1) * head_cols].T) for group in range(GROUPS)])
    patch_grad = patch_total.astype(jnp.bfloat16)
    input_grad = (residual_grad + norm_backward(byte_float, attention_gain, normed_bytes_grad)).astype(jnp.bfloat16)
    grad_query = matmul_plain(normed_bytes.T, query_grad)
    grad_key = matmul_plain(patch_states.T, key_grad)
    grad_value = matmul_plain(patch_states.T, value_grad)
    grad_output = matmul_plain(attended.T, residual_half)
    grad_gate = matmul_plain(normed_hidden.T, gate_grad)
    grad_up = matmul_plain(normed_hidden.T, up_grad)
    grad_down = matmul_plain(hidden.T, cotangent)
    flat_rows = []
    for group in range(GROUPS):
        head_lo = group * head_cols
        head_hi = head_lo + head_cols
        unit_lo = group * unit_cols
        unit_hi = unit_lo + unit_cols
        pieces = [grad_query[:, head_lo:head_hi], grad_key[:, head_lo:head_hi], grad_value[:, head_lo:head_hi], grad_output[head_lo:head_hi, :], grad_gate[:, unit_lo:unit_hi], grad_up[:, unit_lo:unit_hi], grad_down[unit_lo:unit_hi, :]]
        flat_rows.append(jnp.concatenate([piece.reshape(N_DP, -1) for piece in pieces], axis=1).reshape(-1))
    flat_grad = jnp.stack(flat_rows) * TOKENS ** (-0.5)
    new_first = beta_first * adam_first + (1.0 - beta_first) * flat_grad
    new_second = beta_second * adam_second + (1.0 - beta_second) * flat_grad * flat_grad
    adam_step = new_first / bias_first / (jnp.sqrt(new_second / bias_second) + adam_epsilon)
    return (input_grad, patch_grad, new_first, new_second, adam_step)
```

```python
import functools

import jax
import jax.numpy as jnp
from jax import lax
from jax.experimental import pallas as pl
from jax.experimental.pallas import tpu as pltpu
from jax.sharding import PartitionSpec as P

HEAD = 128
BYTES = 512
PATCHES = 128
LANES = 128

norm_epsilon = 1e-05
adam_epsilon = 1e-08
beta_first = 0.9
beta_second = 0.95
score_scale = 0.125
bias_first = 1.0 - 0.9**20
bias_second = 1.0 - 0.95**20


F32 = jnp.float32
BF16 = jnp.bfloat16


def norm_forward(inputs, gain_vec):
    inverse = lax.rsqrt(jnp.mean(inputs * inputs, axis=-1, keepdims=True) + norm_epsilon)
    return inputs * inverse * gain_vec


def norm_backward(inputs, gain_vec, grad_vec):
    inverse = lax.rsqrt(jnp.mean(inputs * inputs, axis=-1, keepdims=True) + norm_epsilon)
    scaled = grad_vec * gain_vec
    inner = jnp.mean(scaled * inputs, axis=-1, keepdims=True)
    return inverse * scaled - inputs * (inverse * inverse * inverse) * inner


def dot(left, right):
    return jnp.dot(left, right, preferred_element_type=F32)


def dot_rt(left, right):
    return lax.dot_general(left, right, (((1,), (1,)), ((), ())), preferred_element_type=F32)


def dot_lt(left, right):
    return lax.dot_general(left, right, (((0,), (0,)), ((), ())), preferred_element_type=F32)


def swap(value, axis, bit):
    size = lax.axis_size(axis)
    return lax.ppermute(value, axis, [(i, i ^ bit) for i in range(size)])


def codes(bits):
    result = [0]
    for bit in reversed(bits):
        result = result + [code | bit for code in result]
    return result


def blocks_in_order(value, index, code_list):
    count = len(code_list)
    rows = value.shape[0] // count
    return [
        lax.dynamic_slice_in_dim(value, (index ^ code) * rows, rows, 0) for code in code_list
    ]


def scatter_sum(blocks, bits):
    for step, bit in enumerate(bits):
        half = blocks.shape[0] // 2
        received = swap(blocks[half:], "dp", bit)
        total = blocks[:half].astype(F32) + received.astype(F32)
        blocks = total if step == len(bits) - 1 else total.astype(BF16)
    return blocks[0].astype(F32)


def adam_kernel(scale, layout, *refs):
    count = len(layout)
    grads = refs[:count]
    first_hbm, second_hbm = refs[count : count + 2]
    new_first_hbm, new_second_hbm, step_hbm = refs[-13:-10]
    first, second, new_first, new_second, step_out = refs[-10:-5]
    sems = refs[-5:]
    start = layout[0][0]
    total = sum(rows * cols for _, rows, cols in layout)
    window = pl.ds(start, total)
    load_first = pltpu.make_async_copy(first_hbm.at[window], first, sems[0])
    load_second = pltpu.make_async_copy(second_hbm.at[window], second, sems[1])
    load_first.start()
    load_second.start()
    load_first.wait()
    load_second.wait()
    for grad_ref, (offset, rows, cols) in zip(grads, layout):
        for col in range(cols):
            at = pl.ds(offset - start + col, rows, stride=cols)
            grad = grad_ref[:, col * LANES : (col + 1) * LANES].astype(F32) * scale
            moment = beta_first * first[at, :] + (1.0 - beta_first) * grad
            square = beta_second * second[at, :] + (1.0 - beta_second) * grad * grad
            new_first[at, :] = moment
            new_second[at, :] = square
            step_out[at, :] = (
                moment / bias_first / (jnp.sqrt(square / bias_second) + adam_epsilon)
            )
    stores = [
        pltpu.make_async_copy(src, dst.at[window], sem)
        for src, dst, sem in zip(
            (new_first, new_second, step_out), (new_first_hbm, new_second_hbm, step_hbm), sems[2:]
        )
    ]
    for store in stores:
        store.start()
    for store in stores:
        store.wait()


def adam_part(grads, start, first, second, previous, scale):
    layout = []
    offset = start
    for grad in grads:
        rows, cols = grad.shape[0], grad.shape[1] // LANES
        layout.append((offset, rows, cols))
        offset += rows * cols
    count = len(grads)
    total = offset - start
    shape = jax.ShapeDtypeStruct(first.shape, F32)
    hbm = pl.BlockSpec(memory_space=pl.ANY)
    vmem = pl.BlockSpec(memory_space=pltpu.VMEM)
    previous = () if previous is None else previous
    aliases = {count + 2 + k: k for k in range(len(previous))}
    outs = pl.pallas_call(
        functools.partial(adam_kernel, scale, tuple(layout)),
        out_shape=(shape,) * 3,
        in_specs=[vmem] * count + [hbm] * (2 + len(previous)),
        out_specs=(hbm,) * 3,
        scratch_shapes=[pltpu.VMEM((total, LANES), F32)] * 5 + [pltpu.SemaphoreType.DMA] * 5,
        input_output_aliases=aliases,
        name="adam",
    )(*grads, first, second, *previous)
    return outs, offset


def shards(
    byte_states,
    patch_states,
    patch_lengths,
    cotangent,
    attention_gain,
    feedforward_gain,
    query_weight,
    key_weight,
    value_weight,
    output_weight,
    gate_weight,
    up_weight,
    down_weight,
    adam_first,
    adam_second,
):
    row_count = byte_states.shape[0]
    n_dp = lax.axis_size("dp")
    n_heads = lax.axis_size("heads")
    dp = lax.axis_index("dp")
    group = lax.axis_index("heads")
    heads_here = query_weight.shape[1] // HEAD
    block = row_count // n_heads
    bits = [1 << k for k in range(n_dp.bit_length() - 1)]
    swapped_bits = bits[1::-1] + bits[2:]
    head_codes = codes([1, 2])
    half = row_count // 2

    byte_half = jnp.concatenate(blocks_in_order(byte_states, group, head_codes))
    cot = jnp.concatenate(blocks_in_order(cotangent, group, head_codes))
    row_base = jnp.arange(block, dtype=jnp.int32)
    positions = jnp.concatenate([(group ^ code) * block + row_base for code in head_codes])

    patch_order = codes(bits)
    width = patch_states.shape[1] // n_dp
    patch_cols = []
    for code in patch_order:
        cut = lax.dynamic_slice_in_dim(patch_states, (dp ^ code) * width, width, 1)
        if code:
            cut = lax.ppermute(cut, "dp", [(i, i ^ code) for i in range(n_dp)])
        patch_cols.append(cut)

    byte_float = byte_half.astype(F32)
    normed_bytes = norm_forward(byte_float, attention_gain).astype(BF16)
    query_full = dot(normed_bytes, query_weight)
    key_full = dot(patch_states, key_weight)
    value_proj = dot(patch_states, value_weight).astype(BF16)
    starts = jnp.cumsum(patch_lengths, axis=1) - patch_lengths
    visible = (starts[0][None, :] <= positions[:, None]).astype(F32)
    heads_q, heads_k, probs, prob_half, attended_parts = [], [], [], [], []
    for head in range(heads_here):
        cols = slice(head * HEAD, (head + 1) * HEAD)
        query_n = norm_forward(query_full[:, cols], 1.0).astype(BF16)
        key_n = norm_forward(key_full[:, cols], 1.0).astype(BF16)
        weights = jnp.exp(score_scale * dot_rt(query_n, key_n)) * visible
        prob = weights / jnp.sum(weights, axis=-1, keepdims=True)
        heads_q.append(query_n)
        heads_k.append(key_n)
        probs.append(prob)
        prob_half.append(prob.astype(BF16))
        attended_parts.append(dot(prob_half[-1], value_proj[:, cols]).astype(BF16))
    attended = jnp.concatenate(attended_parts, axis=1)
    attention_part = dot(attended, output_weight).astype(BF16)

    def half_sum(part):
        near = part[:half].astype(F32) + swap(part[half:], "heads", 1).astype(F32)
        near = near.astype(BF16)
        own, other = near[:block], near[block:]
        own_sum = own.astype(F32) + swap(other, "heads", 2).astype(F32)
        other_sum = other.astype(F32) + swap(own, "heads", 2).astype(F32)
        return jnp.concatenate([own_sum, other_sum])

    residual = byte_float[:half] + half_sum(attention_part)
    normed_half = norm_forward(residual, feedforward_gain).astype(BF16)
    normed_hidden = jnp.concatenate([normed_half, swap(normed_half, "heads", 1)])

    hidden_grad = dot_rt(cot, down_weight)
    gate = dot(normed_hidden, gate_weight)
    up_vals = dot(normed_hidden, up_weight)
    sigmoid = jax.nn.sigmoid(gate)
    activated = gate * sigmoid
    hidden = (activated * up_vals).astype(BF16)
    gate_grad = (hidden_grad * up_vals * (sigmoid * (1.0 + gate * (1.0 - sigmoid)))).astype(BF16)
    up_grad = (hidden_grad * activated).astype(BF16)
    normed_grad_part = (dot_rt(gate_grad, gate_weight) + dot_rt(up_grad, up_weight)).astype(BF16)
    normed_grad = half_sum(normed_grad_part)

    def ordered_t(value, bit_list):
        parts = blocks_in_order(value.T, dp, codes(bit_list))
        return jnp.concatenate(parts)

    def grad_sum(left_t, right, bit_list):
        full = dot(left_t, right).astype(BF16)
        return scatter_sum(full.reshape(n_dp, -1, right.shape[1]), bit_list)

    hidden_cut = cot.shape[1] // 2
    gate_piece = grad_sum(ordered_t(normed_hidden, bits), gate_grad, bits)
    up_piece = grad_sum(ordered_t(normed_hidden, swapped_bits), up_grad, swapped_bits)
    down_piece = jnp.concatenate(
        [
            grad_sum(ordered_t(hidden, bits), cot[:, :hidden_cut], bits),
            grad_sum(ordered_t(hidden, swapped_bits), cot[:, hidden_cut:], swapped_bits),
        ],
        axis=1,
    )

    residual_grad = cot[:half].astype(F32) + norm_backward(residual, feedforward_gain, normed_grad)
    residual_own = residual_grad.astype(BF16)
    residual_half = jnp.concatenate([residual_own, swap(residual_own, "heads", 1)])

    attended_grad = dot_rt(residual_half, output_weight).astype(BF16)
    query_parts, key_parts, value_parts = [], [], []
    for head in range(heads_here):
        cols = slice(head * HEAD, (head + 1) * HEAD)
        prob = probs[head]
        grad_here = attended_grad[:, cols]
        prob_grad = dot_rt(grad_here, value_proj[:, cols])
        score_grad = (
            score_scale
            * prob
            * (prob_grad - jnp.sum(prob * prob_grad, axis=-1, keepdims=True))
        ).astype(BF16)
        query_parts.append(
            norm_backward(query_full[:, cols], 1.0, dot(score_grad, heads_k[head])).astype(BF16)
        )
        key_parts.append(
            norm_backward(key_full[:, cols], 1.0, dot_lt(score_grad, heads_q[head])).astype(BF16)
        )
        value_parts.append(dot_lt(prob_half[head], grad_here).astype(BF16))
    query_grad = jnp.concatenate(query_parts, axis=1)
    patch_side = jnp.concatenate(key_parts + value_parts, axis=1)
    key_cols = key_weight.shape[1]

    bytes_part = dot_rt(query_grad, query_weight).astype(BF16)
    side = jnp.concatenate(blocks_in_order(patch_side, group, head_codes))
    patch_part = (
        dot_rt(side[:, :key_cols], key_weight) + dot_rt(side[:, key_cols:], value_weight)
    ).astype(BF16)

    def row_sum(part):
        rows = part.shape[0] // 2
        near = part[:rows].astype(F32) + swap(part[rows:], "heads", 1).astype(F32)
        near = near.astype(BF16)
        rows = rows // 2
        return near[:rows].astype(F32) + swap(near[rows:], "heads", 2).astype(F32)

    bytes_grad = row_sum(bytes_part)
    patch_grad = row_sum(patch_part).astype(BF16)
    input_grad = (
        residual_grad[:block] + norm_backward(byte_float[:block], attention_gain, bytes_grad)
    ).astype(BF16)

    query_piece = grad_sum(ordered_t(normed_bytes, bits), query_grad, bits)
    output_piece = grad_sum(ordered_t(attended, swapped_bits), residual_half, swapped_bits)
    gathered = patch_side[None]
    for bit in reversed(bits):
        gathered = jnp.concatenate([gathered, swap(gathered, "dp", bit)])
    gathered = gathered.reshape(-1, gathered.shape[-1])
    columns = jnp.concatenate(patch_cols)
    patch_piece = dot_lt(columns, gathered)
    key_piece, value_piece = patch_piece[:, :key_cols], patch_piece[:, key_cols:]

    scale = float(row_count * n_dp) ** (-0.5)
    first = adam_first.reshape(-1, LANES)
    second = adam_second.reshape(-1, LANES)
    outs, at = adam_part(
        [query_piece, key_piece, value_piece, output_piece], 0, first, second, None, scale
    )
    for piece in (gate_piece, up_piece, down_piece):
        outs, at = adam_part([piece], at, first, second, outs, scale)
    outs = tuple(out.reshape(1, -1) for out in outs)
    return (input_grad, patch_grad) + outs


def solution(mesh):
    placed = (
        P("dp", None),
        P("dp", None),
        P("dp", None),
        P("dp", None),
        P(),
        P(),
        P(None, "heads"),
        P(None, "heads"),
        P(None, "heads"),
        P("heads", None),
        P(None, "heads"),
        P(None, "heads"),
        P("heads", None),
        P("heads", "dp"),
        P("heads", "dp"),
    )
    return jax.shard_map(
        shards,
        mesh=mesh,
        in_specs=placed,
        out_specs=(
            P(("dp", "heads"), None),
            P(("dp", "heads"), None),
            P("heads", "dp"),
            P("heads", "dp"),
            P("heads", "dp"),
        ),
        check_vma=False,
    )
```

```python
import functools

import jax
import jax.numpy as jnp
from jax import lax
from jax.experimental import pallas as pl
from jax.experimental.pallas import tpu as pltpu
from jax.sharding import PartitionSpec as P

HEAD = 128
BYTES = 512
PATCHES = 128
LANES = 128

norm_epsilon = 1e-05
adam_epsilon = 1e-08
beta_first = 0.9
beta_second = 0.95
score_scale = 0.125
bias_first = 1.0 - 0.9**20
bias_second = 1.0 - 0.95**20


F32 = jnp.float32
BF16 = jnp.bfloat16


def norm_forward(inputs, gain_vec):
    inverse = lax.rsqrt(jnp.mean(inputs * inputs, axis=-1, keepdims=True) + norm_epsilon)
    return inputs * inverse * gain_vec


def norm_backward(inputs, gain_vec, grad_vec):
    inverse = lax.rsqrt(jnp.mean(inputs * inputs, axis=-1, keepdims=True) + norm_epsilon)
    scaled = grad_vec * gain_vec
    inner = jnp.mean(scaled * inputs, axis=-1, keepdims=True)
    return inverse * scaled - inputs * (inverse * inverse * inverse) * inner


def dot(left, right):
    return jnp.dot(left, right, preferred_element_type=F32)


def dot_rt(left, right):
    return lax.dot_general(left, right, (((1,), (1,)), ((), ())), preferred_element_type=F32)


def dot_lt(left, right):
    return lax.dot_general(left, right, (((0,), (0,)), ((), ())), preferred_element_type=F32)


def swap(value, axis, bit):
    size = lax.axis_size(axis)
    return lax.ppermute(value, axis, [(i, i ^ bit) for i in range(size)])


def codes(bits):
    result = [0]
    for bit in reversed(bits):
        result = result + [code | bit for code in result]
    return result


def vmem_call(kernel, outs, *args, name, smem=0, prefetch=(), hbm=()):
    specs = [pl.BlockSpec(memory_space=pltpu.SMEM)] * smem
    specs += [pl.BlockSpec(memory_space=pltpu.VMEM)] * (len(args) - smem)
    for index in hbm:
        specs[index] = pl.BlockSpec(memory_space=pl.ANY)
    return pl.pallas_call(
        kernel,
        out_shape=tuple(jax.ShapeDtypeStruct(shape, dtype) for shape, dtype in outs),
        in_specs=specs,
        out_specs=(pl.BlockSpec(memory_space=pltpu.VMEM),) * len(outs),
        name=name,
    )(*args)


def scatter_rest(keep, send, bits):
    for step, bit in enumerate(bits):
        received = swap(send, "dp", bit)
        if step == len(bits) - 1:
            return keep, received
        keep, send = add_halves(keep, received)


def add_halves_kernel(left, right, keep, send):
    rows = keep.shape[0]
    keep[...] = (left[:rows].astype(F32) + right[:rows].astype(F32)).astype(BF16)
    send[...] = (left[rows:].astype(F32) + right[rows:].astype(F32)).astype(BF16)


def add_halves(left, right):
    rows, cols = left.shape
    if rows % 32:
        total = (left.astype(F32) + right.astype(F32)).astype(BF16)
        return total[: rows // 2], total[rows // 2 :]
    half = ((rows // 2, cols), BF16)
    return vmem_call(add_halves_kernel, [half, half], left, right, name="add_halves")


def add_kernel(left, right, total):
    total[...] = (left[...].astype(F32) + right[...].astype(F32)).astype(BF16)


def add(left, right):
    return vmem_call(add_kernel, [(left.shape, BF16)], left, right, name="add")[0]


def rows_kernel(code_list, group, source, *rest):
    out = rest[-1]
    rows = out.shape[0] // len(code_list)
    for position, code in enumerate(code_list):
        start = pl.multiple_of((group[0] ^ code) * rows, rows)
        out[position * rows : (position + 1) * rows, :] = source[pl.ds(start, rows), :]


def rows_in_order(source, group, code_list, after):
    kernel = functools.partial(rows_kernel, code_list)
    return vmem_call(
        kernel, [(source.shape, source.dtype)], group, source, after,
        name="rows", smem=1, hbm=(2,),
    )[0]


def attention_kernel(
    code_list, heads, group, bytes_in, patch, lengths, gain, wq, wk, wv, wo,
    bytes_half, normed, query_full, key_full, value, query_n, key_n, probs, attended, keep, send,
):
    count = len(code_list)
    block = bytes_in.shape[0] // count
    half = keep.shape[0]
    key_all = dot(patch[...], wk[...])
    key_full[...] = key_all
    value_all = dot(patch[...], wv[...]).astype(BF16)
    value[...] = value_all
    before = lax.broadcasted_iota(jnp.int32, (PATCHES, PATCHES), 0)
    after = lax.broadcasted_iota(jnp.int32, (PATCHES, PATCHES), 1)
    lower = (before < after).astype(F32).astype(BF16)
    spread = jnp.broadcast_to(lengths[...].astype(F32), (16, PATCHES)).astype(BF16)
    starts = dot(spread, lower)[0:1, :]
    for position, code in enumerate(code_list):
        here = slice(position * block, (position + 1) * block)
        start = pl.multiple_of((group[0] ^ code) * block, block)
        rows = bytes_in[pl.ds(start, block), :]
        if (position + 1) * block <= half:
            bytes_half[here, :] = rows
        normed_rows = norm_forward(rows.astype(F32), gain[...]).astype(BF16)
        normed[here, :] = normed_rows
        query = dot(normed_rows, wq[...])
        query_full[here, :] = query
        place = lax.broadcasted_iota(jnp.int32, (block, 1), 0) + start
        visible = starts <= place.astype(F32)
        for head in range(heads):
            cols = slice(head * HEAD, (head + 1) * HEAD)
            query_here = norm_forward(query[:, cols], 1.0).astype(BF16)
            query_n[here, cols] = query_here
            key_here = norm_forward(key_all[:, cols], 1.0).astype(BF16)
            if position == 0:
                key_n[:, cols] = key_here
            weights = jnp.exp(score_scale * dot_rt(query_here, key_here))
            weights = jnp.where(visible, weights, 0.0)
            prob = weights / jnp.sum(weights, axis=-1, keepdims=True)
            probs[head, here, :] = prob
            attended[here, cols] = dot(prob.astype(BF16), value_all[:, cols]).astype(BF16)
    send[...] = dot(attended[half:, :], wo[...]).astype(BF16)
    keep[...] = dot(attended[:half, :], wo[...]).astype(BF16)


def residual_kernel(bytes_half, near, far, gain, residual, normed):
    rows = near.shape[0] // 2
    for here, there in ((slice(0, rows), slice(rows, None)), (slice(rows, None), slice(0, rows))):
        total = near[here, :].astype(F32) + far[there, :].astype(F32)
        total = bytes_half[here, :].astype(F32) + total
        residual[here, :] = total
        normed[here, :] = norm_forward(total, gain[...]).astype(BF16)


def feedforward_kernel(normed, hidden_grad, gate_w, up_w, gate_g, up_g, hidden, *part):
    width = gate_w.shape[1]
    step = 2 * LANES
    for low in range(0, width, step):
        cols = slice(low, min(low + step, width))
        gate = dot(normed[...], gate_w[:, cols])
        up = dot(normed[...], up_w[:, cols])
        grad = hidden_grad[:, cols]
        sigmoid = jax.nn.sigmoid(gate)
        activated = gate * sigmoid
        hidden[:, cols] = (activated * up).astype(BF16)
        gate_g[:, cols] = (grad * up * (sigmoid * (1.0 + gate * (1.0 - sigmoid)))).astype(BF16)
        up_g[:, cols] = (grad * activated).astype(BF16)
    if part:
        part[0][...] = (
            dot_rt(gate_g[...], gate_w[...]) + dot_rt(up_g[...], up_w[...])
        ).astype(BF16)


def feedforward(normed, hidden_grad, gate_w, up_w, with_part):
    rows, width = hidden_grad.shape
    outs = [((rows, width), BF16)] * 3
    if with_part:
        outs.append((normed.shape, BF16))
    return vmem_call(
        feedforward_kernel, outs, normed, hidden_grad, gate_w, up_w, name="feedforward"
    )


def residual_grad_kernel(residual, cot, near, far, gain, grad_out, half_out):
    rows = near.shape[0] // 2
    for first, here, there in (
        (True, slice(0, rows), slice(rows, None)),
        (False, slice(rows, None), slice(0, rows)),
    ):
        total = near[here, :].astype(F32) + far[there, :].astype(F32)
        grad = cot[here, :].astype(F32) + norm_backward(residual[here, :], gain[...], total)
        if first:
            grad_out[...] = grad
        half_out[here, :] = grad.astype(BF16)


def attention_grad_kernel(
    heads, own, other, wo, value, key_n, query_n, probs, query_full, key_full, wq,
    query_grad, side, keep, send,
):
    half = own.shape[0]
    own_grad = dot_rt(own[...], wo[...]).astype(BF16)
    other_grad = dot_rt(other[...], wo[...]).astype(BF16)
    for head in range(heads):
        cols = slice(head * HEAD, (head + 1) * HEAD)
        key_total = value_total = None
        for here, grads in ((slice(0, half), own_grad), (slice(half, None), other_grad)):
            prob = probs[head, here, :]
            grad_here = grads[:, cols]
            prob_grad = dot_rt(grad_here, value[:, cols])
            inner = jnp.sum(prob * prob_grad, axis=-1, keepdims=True)
            score_grad = (score_scale * prob * (prob_grad - inner)).astype(BF16)
            query_ng = dot(score_grad, key_n[:, cols])
            query_grad[here, cols] = norm_backward(query_full[here, cols], 1.0, query_ng).astype(
                BF16
            )
            key_term = dot_lt(score_grad, query_n[here, cols])
            value_term = dot_lt(prob.astype(BF16), grad_here)
            key_total = key_term if key_total is None else key_total + key_term
            value_total = value_term if value_total is None else value_total + value_term
        side[:, cols] = norm_backward(key_full[:, cols], 1.0, key_total).astype(BF16)
        shifted = slice((heads + head) * HEAD, (heads + head + 1) * HEAD)
        side[:, shifted] = value_total.astype(BF16)
    send[...] = dot_rt(query_grad[half:, :], wq[...]).astype(BF16)
    keep[...] = dot_rt(query_grad[:half, :], wq[...]).astype(BF16)


def patch_grad_kernel(code_list, group, side, wk, wv, keep, send):
    rows = side.shape[0] // len(code_list)
    cols = wk.shape[1]
    parts = []
    for code in code_list:
        start = pl.multiple_of((group[0] ^ code) * rows, rows)
        parts.append(side[pl.ds(start, rows), :])
    ordered = jnp.concatenate(parts, axis=0)
    total = dot_rt(ordered[:, :cols], wk[...]) + dot_rt(ordered[:, cols:], wv[...])
    half = keep.shape[0]
    keep[...] = total[:half].astype(BF16)
    send[...] = total[half:].astype(BF16)


def input_grad_kernel(residual_grad, bytes_half, near, far, gain, out):
    rows = out.shape[0]
    total = near[:rows].astype(F32) + far[...].astype(F32)
    states = bytes_half[:rows].astype(F32)
    out[...] = (residual_grad[...] + norm_backward(states, gain[...], total)).astype(BF16)


def pick_kernel(code_list, rows, index, *refs):
    sources, out, turned = refs[:-2], refs[-2], refs[-1]
    low = 0
    for source in sources:
        high = low + source.shape[0]
        turned[:, low:high] = source[...].T
        low = high
    for position, code in enumerate(code_list):
        start = pl.multiple_of((index[0] ^ code) * rows, rows)
        out[position * rows : (position + 1) * rows, :] = turned[pl.ds(start, rows), :]


def pick_transposed(sources, index, count, code_list):
    width = sources[0].shape[1]
    rows = width // count
    total = sum(source.shape[0] for source in sources)
    if rows % 16:
        turned = jnp.concatenate(sources).T
        return jnp.concatenate(
            [
                lax.dynamic_slice_in_dim(turned, (index[0] ^ code) * rows, rows, 0)
                for code in code_list
            ]
        )
    return pl.pallas_call(
        functools.partial(pick_kernel, code_list, rows),
        out_shape=jax.ShapeDtypeStruct((rows * len(code_list), total), BF16),
        in_specs=[pl.BlockSpec(memory_space=pltpu.SMEM)]
        + [pl.BlockSpec(memory_space=pltpu.VMEM)] * len(sources),
        out_specs=pl.BlockSpec(memory_space=pltpu.VMEM),
        scratch_shapes=[pltpu.VMEM((width, total), BF16)],
        name="pick",
    )(index, *sources)


def weight_grad_kernel(left, *refs):
    rights, (keep, send) = refs[:-2], refs[-2:]
    half = keep.shape[0]
    for out, rows in ((send, slice(half, None)), (keep, slice(0, half))):
        total, low = None, 0
        for right in rights:
            high = low + right.shape[0]
            term = dot(left[rows, low:high], right[...])
            total = term if total is None else total + term
            low = high
        out[...] = total.astype(BF16)


def weight_grad(left, rights):
    half = ((left.shape[0] // 2, rights[0].shape[1]), BF16)
    return vmem_call(weight_grad_kernel, [half, half], left, *rights, name="weight_grad")


def adam_kernel(scale, layout, spans, *refs):
    count = len(layout)
    terms = []
    taken = 0
    for width in spans:
        terms.append(refs[taken : taken + width])
        taken += width
    first_hbm, second_hbm = refs[taken : taken + 2]
    new_first_hbm, new_second_hbm, step_hbm = refs[-13:-10]
    first, second, new_first, new_second, step_out = refs[-10:-5]
    sems = refs[-5:]
    start = layout[0][0]
    total = sum(rows * cols for _, rows, cols, _ in layout)
    window = pl.ds(start, total)
    load_first = pltpu.make_async_copy(first_hbm.at[window], first, sems[0])
    load_second = pltpu.make_async_copy(second_hbm.at[window], second, sems[1])
    load_first.start()
    load_second.start()
    load_first.wait()
    load_second.wait()
    for refs_here, (offset, rows, cols, pick) in zip(terms, layout):
        for col in range(cols):
            at = pl.ds(offset - start + col, rows, stride=cols)
            grad = None
            for ref in refs_here:
                term = pick(ref, col).astype(F32)
                grad = term if grad is None else grad + term
            grad = grad * scale
            moment = beta_first * first[at, :] + (1.0 - beta_first) * grad
            square = beta_second * second[at, :] + (1.0 - beta_second) * grad * grad
            new_first[at, :] = moment
            new_second[at, :] = square
            step_out[at, :] = (
                moment / bias_first / (jnp.sqrt(square / bias_second) + adam_epsilon)
            )
    stores = [
        pltpu.make_async_copy(src, dst.at[window], sem)
        for src, dst, sem in zip(
            (new_first, new_second, step_out), (new_first_hbm, new_second_hbm, step_hbm), sems[2:]
        )
    ]
    for store in stores:
        store.start()
    for store in stores:
        store.wait()


def natural(ref, col):
    return ref[:, col * LANES : (col + 1) * LANES]


def adam_part(parts, start, first, second, previous, scale):
    layout, arrays, spans = [], [], []
    offset = start
    for terms, rows, cols, pick in parts:
        layout.append((offset, rows, cols, pick))
        arrays += terms
        spans.append(len(terms))
        offset += rows * cols
    count = len(arrays)
    total = offset - start
    shape = jax.ShapeDtypeStruct(first.shape, F32)
    hbm = pl.BlockSpec(memory_space=pl.ANY)
    vmem = pl.BlockSpec(memory_space=pltpu.VMEM)
    previous = () if previous is None else previous
    aliases = {count + 2 + k: k for k in range(len(previous))}
    outs = pl.pallas_call(
        functools.partial(adam_kernel, scale, tuple(layout), tuple(spans)),
        out_shape=(shape,) * 3,
        in_specs=[vmem] * count + [hbm] * (2 + len(previous)),
        out_specs=(hbm,) * 3,
        scratch_shapes=[pltpu.VMEM((total, LANES), F32)] * 5 + [pltpu.SemaphoreType.DMA] * 5,
        input_output_aliases=aliases,
        name="adam",
    )(*arrays, first, second, *previous)
    return outs, offset


def pair_grad_kernel(normed_t, query_grad, attended_t, own, other, keep, send, count):
    rows_q = normed_t.shape[0] // count
    rows_o = attended_t.shape[0] // count
    width = keep.shape[1]
    half = own.shape[0]
    query_all = dot(normed_t[...], query_grad[...]).astype(BF16)
    output_all = (
        dot(attended_t[:, :half], own[...]) + dot(attended_t[:, half:], other[...])
    ).astype(BF16)
    rows = rows_q + own.shape[1] // width * rows_o
    for position in range(count):
        out = keep if position < count // 2 else send
        low = position % (count // 2) * rows
        out[low : low + rows_q, :] = query_all[position * rows_q : (position + 1) * rows_q]
        low += rows_q
        for piece in range(own.shape[1] // width):
            out[low : low + rows_o, :] = output_all[
                position * rows_o : (position + 1) * rows_o, piece * width : (piece + 1) * width
            ]
            low += rows_o


def shards(
    byte_states,
    patch_states,
    patch_lengths,
    cotangent,
    attention_gain,
    feedforward_gain,
    query_weight,
    key_weight,
    value_weight,
    output_weight,
    gate_weight,
    up_weight,
    down_weight,
    adam_first,
    adam_second,
):
    row_count, model = byte_states.shape
    n_dp = lax.axis_size("dp")
    n_heads = lax.axis_size("heads")
    dp = lax.axis_index("dp").astype(jnp.int32)
    dp_index = dp.reshape(1)
    group = lax.axis_index("heads").astype(jnp.int32).reshape(1)
    head_cols = query_weight.shape[1]
    heads = head_cols // HEAD
    hidden_here = gate_weight.shape[1]
    block = row_count // n_heads
    half = row_count // 2
    bits = [1 << k for k in range(n_dp.bit_length() - 1)]
    pair, rest = bits[0], bits[1:]
    head_codes = codes([1, 2])
    attention_row = attention_gain.reshape(1, -1)
    feedforward_row = feedforward_gain.reshape(1, -1)

    part_shape = ((half, model), BF16)
    (
        bytes_half, normed_bytes, query_full, key_full, value, query_n, key_n, probs, attended,
        keep, send,
    ) = vmem_call(
        functools.partial(attention_kernel, head_codes, heads),
        [
            part_shape,
            ((row_count, model), BF16),
            ((row_count, head_cols), F32),
            ((PATCHES, head_cols), F32),
            ((PATCHES, head_cols), BF16),
            ((row_count, head_cols), BF16),
            ((PATCHES, head_cols), BF16),
            ((heads, row_count, PATCHES), F32),
            ((row_count, head_cols), BF16),
            part_shape,
            part_shape,
        ],
        group, byte_states, patch_states, patch_lengths, attention_row,
        query_weight, key_weight, value_weight, output_weight,
        name="attention", smem=1,
    )
    near = add(keep, swap(send, "heads", 1))
    far = swap(near, "heads", 2)

    cot = rows_in_order(cotangent, group, head_codes, near)
    cot_own, cot_other = cot[:half], cot[half:]
    cot_pair_own = swap(cot_own, "dp", pair)
    hidden_grad = dot_rt(cot, down_weight)

    residual, normed_own = vmem_call(
        residual_kernel,
        [((half, model), F32), part_shape],
        bytes_half, near, far, feedforward_row,
        name="residual",
    )
    normed_other = swap(normed_own, "heads", 1)
    normed_pair_own = swap(normed_own, "dp", pair)
    gate_own, up_own, hidden_own, part_own = feedforward(
        normed_own, hidden_grad[:half], gate_weight, up_weight, True
    )
    gate_other, up_other, hidden_other, part_other = feedforward(
        normed_other, hidden_grad[half:], gate_weight, up_weight, True
    )
    near = add(part_own, swap(part_other, "heads", 1))
    far = swap(near, "heads", 2)

    cot_pair_other = swap(cot_pair_own, "heads", 1)
    cot_pair = jnp.concatenate([cot_pair_own, cot_pair_other])
    hidden_grad_pair = dot_rt(cot_pair, down_weight)
    normed_pair_other = swap(normed_pair_own, "heads", 1)
    normed_pair = jnp.concatenate([normed_pair_own, normed_pair_other])
    gate_pair, up_pair, hidden_pair = feedforward(
        normed_pair, hidden_grad_pair, gate_weight, up_weight, False
    )
    rest_codes = codes(rest)
    normed_t = pick_transposed(
        [normed_own, normed_other, normed_pair], dp_index, n_dp, rest_codes
    )
    hidden_t = pick_transposed(
        [hidden_own, hidden_other, hidden_pair], dp_index, n_dp, rest_codes
    )
    gate_terms = scatter_rest(*weight_grad(normed_t, [gate_own, gate_other, gate_pair]), rest)
    up_terms = scatter_rest(*weight_grad(normed_t, [up_own, up_other, up_pair]), rest)
    down_terms = scatter_rest(*weight_grad(hidden_t, [cot, cot_pair]), rest)

    residual_grad, own = vmem_call(
        residual_grad_kernel,
        [((block, model), F32), part_shape],
        residual, cot_own, near, far, feedforward_row,
        name="residual_grad",
    )
    other = swap(own, "heads", 1)

    query_grad, side, keep, send = vmem_call(
        functools.partial(attention_grad_kernel, heads),
        [
            ((row_count, head_cols), BF16),
            ((PATCHES, 2 * head_cols), BF16),
            part_shape,
            part_shape,
        ],
        own, other, output_weight, value, key_n, query_n, probs, query_full, key_full,
        query_weight,
        name="attention_grad",
    )
    near = add(keep, swap(send, "heads", 1))
    far = swap(near[block:], "heads", 2)
    patch_half = ((PATCHES // 2, patch_states.shape[1]), BF16)
    keep, send = vmem_call(
        functools.partial(patch_grad_kernel, head_codes),
        [patch_half, patch_half],
        group, side, key_weight, value_weight,
        name="patch_grad", smem=1,
    )
    patch_near, patch_send = add_halves(keep, swap(send, "heads", 1))
    patch_grad = add(patch_near, swap(patch_send, "heads", 2))
    (input_grad,) = vmem_call(
        input_grad_kernel,
        [((block, model), BF16)],
        residual_grad, bytes_half, near, far, attention_row,
        name="input_grad",
    )

    patch_order = codes(rest[::-1] + [pair])
    gathered = side
    for bit in rest[::-1] + [pair]:
        gathered = jnp.concatenate([gathered, swap(gathered, "dp", bit)])
    width = patch_states.shape[1] // n_dp
    columns = jnp.stack(
        [
            lax.dynamic_slice_in_dim(patch_states, (dp ^ code) * width, width, 1)
            for code in codes(bits)
        ]
    )
    for step in range(len(bits)):
        columns = columns.reshape(1 << step, -1, PATCHES, width) if step else columns[None]
        split = columns.shape[1] // 2
        received = swap(columns[:, split:], "dp", bits[step])
        columns = jnp.concatenate([columns[:, :split], received], axis=0)
    columns = columns.reshape(-1, width)
    gather_codes = [0]
    for bit in rest[::-1] + [pair]:
        gather_codes = gather_codes + [code | bit for code in gather_codes]
    column_codes = [0]
    for bit in bits:
        column_codes = column_codes + [code | bit for code in column_codes]
    places = [gather_codes.index(code) for code in column_codes]
    gathered = jnp.concatenate(
        [gathered[place * PATCHES : (place + 1) * PATCHES] for place in places]
    )
    patch_piece = dot_lt(columns, gathered)

    pair_codes = codes(bits)
    normed_bytes_t = pick_transposed([normed_bytes], dp_index, n_dp, pair_codes)
    attended_t = pick_transposed([attended], dp_index, n_dp, pair_codes)
    rows_q, rows_o = model // n_dp, head_cols // n_dp
    rows_both = rows_q + model // head_cols * rows_o
    chain = ((rows_both * n_dp // 2, head_cols), BF16)
    keep, send = vmem_call(
        functools.partial(pair_grad_kernel, count=n_dp),
        [chain, chain],
        normed_bytes_t, query_grad, attended_t, own, other,
        name="pair_grad",
    )
    pair_terms = list(scatter_rest(keep, send, bits))

    def query_at(ref, col):
        return ref[:rows_q, col * LANES : (col + 1) * LANES]

    def output_at(ref, col):
        per = head_cols // LANES
        low = rows_q + col // per * rows_o
        return ref[low : low + rows_o, col % per * LANES : (col % per + 1) * LANES]

    def key_at(ref, col):
        return ref[:, col * LANES : (col + 1) * LANES]

    def value_at(ref, col):
        return ref[:, head_cols + col * LANES : head_cols + (col + 1) * LANES]

    scale = float(row_count * n_dp) ** (-0.5)
    first = adam_first.reshape(-1, LANES)
    second = adam_second.reshape(-1, LANES)
    per = head_cols // LANES
    outs, at = adam_part(
        [
            (pair_terms, rows_q, per, query_at),
            ([patch_piece], width, per, key_at),
            ([patch_piece], width, per, value_at),
            (pair_terms, rows_o, model // LANES, output_at),
        ],
        0, first, second, None, scale,
    )
    for terms, cols in ((gate_terms, hidden_here), (up_terms, hidden_here), (down_terms, model)):
        rows = terms[0].shape[0]
        outs, at = adam_part(
            [(list(terms), rows, cols // LANES, natural)], at, first, second, outs, scale
        )
    outs = tuple(out.reshape(1, -1) for out in outs)
    return (input_grad, patch_grad) + outs


def solution(mesh):
    placed = (
        P("dp", None),
        P("dp", None),
        P("dp", None),
        P("dp", None),
        P(),
        P(),
        P(None, "heads"),
        P(None, "heads"),
        P(None, "heads"),
        P("heads", None),
        P(None, "heads"),
        P(None, "heads"),
        P("heads", None),
        P("heads", "dp"),
        P("heads", "dp"),
    )
    return jax.shard_map(
        shards,
        mesh=mesh,
        in_specs=placed,
        out_specs=(
            P(("dp", "heads"), None),
            P(("dp", "heads"), None),
            P("heads", "dp"),
            P("heads", "dp"),
            P("heads", "dp"),
        ),
        check_vma=False,
    )
```

```python
import functools
import math

import jax
import jax.numpy as jnp
from jax import lax
from jax.experimental import pallas as pl
from jax.experimental.pallas import tpu as pltpu
from jax.sharding import PartitionSpec as P

HEAD = 128
BYTES = 512
PATCHES = 128
LANES = 128

norm_epsilon = 1e-05
adam_epsilon = 1e-08
beta_first = 0.9
beta_second = 0.95
score_scale = 0.125
bias_first = 1.0 - 0.9**20
bias_second = 1.0 - 0.95**20


F32 = jnp.float32
BF16 = jnp.bfloat16


def norm_forward(inputs, gain_vec):
    inverse = lax.rsqrt(jnp.mean(inputs * inputs, axis=-1, keepdims=True) + norm_epsilon)
    return inputs * inverse * gain_vec


def norm_backward(inputs, gain_vec, grad_vec):
    inverse = lax.rsqrt(jnp.mean(inputs * inputs, axis=-1, keepdims=True) + norm_epsilon)
    scaled = grad_vec * gain_vec
    inner = jnp.mean(scaled * inputs, axis=-1, keepdims=True)
    return inverse * scaled - inputs * (inverse * inverse * inverse) * inner


def dot(left, right):
    return jnp.dot(left, right, preferred_element_type=F32)


def dot_rt(left, right):
    return lax.dot_general(left, right, (((1,), (1,)), ((), ())), preferred_element_type=F32)


def dot_lt(left, right):
    return lax.dot_general(left, right, (((0,), (0,)), ((), ())), preferred_element_type=F32)


def swap(value, axis, bit):
    size = lax.axis_size(axis)
    return lax.ppermute(value, axis, [(i, i ^ bit) for i in range(size)])


def codes(bits):
    result = [0]
    for bit in reversed(bits):
        result = result + [code | bit for code in result]
    return result


def room(outs, args, scratch=0):
    total = sum(math.prod(shape) * jnp.dtype(dtype).itemsize for shape, dtype in outs)
    total += sum(arg.size * arg.dtype.itemsize for arg in args)
    return pltpu.CompilerParams(vmem_limit_bytes=total + total // 8 + scratch + (4 << 20))


def vmem_call(kernel, outs, *args, name, smem=0, prefetch=(), hbm=()):
    specs = [pl.BlockSpec(memory_space=pltpu.SMEM)] * smem
    specs += [pl.BlockSpec(memory_space=pltpu.VMEM)] * (len(args) - smem)
    for index in hbm:
        specs[index] = pl.BlockSpec(memory_space=pl.ANY)
    return pl.pallas_call(
        kernel,
        out_shape=tuple(jax.ShapeDtypeStruct(shape, dtype) for shape, dtype in outs),
        in_specs=specs,
        out_specs=(pl.BlockSpec(memory_space=pltpu.VMEM),) * len(outs),
        compiler_params=room(outs, args),
        name=name,
    )(*args)


def scatter_rest(keep, send, bits):
    for step, bit in enumerate(bits):
        received = swap(send, "dp", bit)
        if step == len(bits) - 1:
            return keep, received
        keep, send = add_halves(keep, received)


def add_halves_kernel(left, right, keep, send):
    rows = keep.shape[0]
    keep[...] = (left[:rows].astype(F32) + right[:rows].astype(F32)).astype(BF16)
    send[...] = (left[rows:].astype(F32) + right[rows:].astype(F32)).astype(BF16)


def add_halves(left, right):
    rows, cols = left.shape
    if rows % 32:
        total = (left.astype(F32) + right.astype(F32)).astype(BF16)
        return total[: rows // 2], total[rows // 2 :]
    half = ((rows // 2, cols), BF16)
    return vmem_call(add_halves_kernel, [half, half], left, right, name="add_halves")


def add_kernel(left, right, total):
    total[...] = (left[...].astype(F32) + right[...].astype(F32)).astype(BF16)


def add(left, right):
    return vmem_call(add_kernel, [(left.shape, BF16)], left, right, name="add")[0]


def rows_kernel(code_list, group, source, *rest):
    out = rest[-1]
    rows = out.shape[0] // len(code_list)
    for position, code in enumerate(code_list):
        start = pl.multiple_of((group[0] ^ code) * rows, rows)
        out[position * rows : (position + 1) * rows, :] = source[pl.ds(start, rows), :]


def rows_in_order(source, group, code_list, after):
    kernel = functools.partial(rows_kernel, code_list)
    return vmem_call(
        kernel, [(source.shape, source.dtype)], group, source, after,
        name="rows", smem=1, hbm=(2,),
    )[0]


def attention_kernel(
    code_list, heads, group, bytes_in, patch, lengths, gain, wq, wk, wv, wo,
    bytes_half, normed, query_full, key_full, value, query_n, key_n, probs, attended, keep, send,
):
    count = len(code_list)
    block = bytes_in.shape[0] // count
    half = keep.shape[0]
    key_all = dot(patch[...], wk[...])
    key_full[...] = key_all
    value_all = dot(patch[...], wv[...]).astype(BF16)
    value[...] = value_all
    before = lax.broadcasted_iota(jnp.int32, (PATCHES, PATCHES), 0)
    after = lax.broadcasted_iota(jnp.int32, (PATCHES, PATCHES), 1)
    lower = (before < after).astype(F32).astype(BF16)
    spread = jnp.broadcast_to(lengths[...].astype(F32), (16, PATCHES)).astype(BF16)
    starts = dot(spread, lower)[0:1, :]
    for position, code in enumerate(code_list):
        here = slice(position * block, (position + 1) * block)
        start = pl.multiple_of((group[0] ^ code) * block, block)
        rows = bytes_in[pl.ds(start, block), :]
        if (position + 1) * block <= half:
            bytes_half[here, :] = rows
        normed_rows = norm_forward(rows.astype(F32), gain[...]).astype(BF16)
        normed[here, :] = normed_rows
        query = dot(normed_rows, wq[...])
        query_full[here, :] = query
        place = lax.broadcasted_iota(jnp.int32, (block, 1), 0) + start
        visible = starts <= place.astype(F32)
        for head in range(heads):
            cols = slice(head * HEAD, (head + 1) * HEAD)
            query_here = norm_forward(query[:, cols], 1.0).astype(BF16)
            query_n[here, cols] = query_here
            key_here = norm_forward(key_all[:, cols], 1.0).astype(BF16)
            if position == 0:
                key_n[:, cols] = key_here
            weights = jnp.exp(score_scale * dot_rt(query_here, key_here))
            weights = jnp.where(visible, weights, 0.0)
            prob = weights / jnp.sum(weights, axis=-1, keepdims=True)
            probs[head, here, :] = prob
            attended[here, cols] = dot(prob.astype(BF16), value_all[:, cols]).astype(BF16)
    send[...] = dot(attended[half:, :], wo[...]).astype(BF16)
    keep[...] = dot(attended[:half, :], wo[...]).astype(BF16)


def residual_kernel(bytes_half, near, far, gain, residual, normed):
    rows = near.shape[0] // 2
    for here, there in ((slice(0, rows), slice(rows, None)), (slice(rows, None), slice(0, rows))):
        total = near[here, :].astype(F32) + far[there, :].astype(F32)
        total = bytes_half[here, :].astype(F32) + total
        residual[here, :] = total
        normed[here, :] = norm_forward(total, gain[...]).astype(BF16)


def feedforward_kernel(normed, hidden_grad, gate_w, up_w, gate_g, up_g, hidden, *part):
    width = gate_w.shape[1]
    step = 2 * LANES
    for low in range(0, width, step):
        cols = slice(low, min(low + step, width))
        gate = dot(normed[...], gate_w[:, cols])
        up = dot(normed[...], up_w[:, cols])
        grad = hidden_grad[:, cols]
        sigmoid = jax.nn.sigmoid(gate)
        activated = gate * sigmoid
        hidden[:, cols] = (activated * up).astype(BF16)
        gate_g[:, cols] = (grad * up * (sigmoid * (1.0 + gate * (1.0 - sigmoid)))).astype(BF16)
        up_g[:, cols] = (grad * activated).astype(BF16)
    if part:
        part[0][...] = (
            dot_rt(gate_g[...], gate_w[...]) + dot_rt(up_g[...], up_w[...])
        ).astype(BF16)


def feedforward(normed, hidden_grad, gate_w, up_w, with_part):
    rows, width = hidden_grad.shape
    outs = [((rows, width), BF16)] * 3
    if with_part:
        outs.append((normed.shape, BF16))
    return vmem_call(
        feedforward_kernel, outs, normed, hidden_grad, gate_w, up_w, name="feedforward"
    )


def residual_grad_kernel(residual, cot, near, far, gain, grad_out, half_out):
    rows = near.shape[0] // 2
    for first, here, there in (
        (True, slice(0, rows), slice(rows, None)),
        (False, slice(rows, None), slice(0, rows)),
    ):
        total = near[here, :].astype(F32) + far[there, :].astype(F32)
        grad = cot[here, :].astype(F32) + norm_backward(residual[here, :], gain[...], total)
        if first:
            grad_out[...] = grad
        half_out[here, :] = grad.astype(BF16)


def attention_grad_kernel(
    heads, own, other, wo, value, key_n, query_n, probs, query_full, key_full, wq,
    query_grad, side, keep, send,
):
    half = own.shape[0]
    own_grad = dot_rt(own[...], wo[...]).astype(BF16)
    other_grad = dot_rt(other[...], wo[...]).astype(BF16)
    for head in range(heads):
        cols = slice(head * HEAD, (head + 1) * HEAD)
        key_total = value_total = None
        for here, grads in ((slice(0, half), own_grad), (slice(half, None), other_grad)):
            prob = probs[head, here, :]
            grad_here = grads[:, cols]
            prob_grad = dot_rt(grad_here, value[:, cols])
            inner = jnp.sum(prob * prob_grad, axis=-1, keepdims=True)
            score_grad = (score_scale * prob * (prob_grad - inner)).astype(BF16)
            query_ng = dot(score_grad, key_n[:, cols])
            query_grad[here, cols] = norm_backward(query_full[here, cols], 1.0, query_ng).astype(
                BF16
            )
            key_term = dot_lt(score_grad, query_n[here, cols])
            value_term = dot_lt(prob.astype(BF16), grad_here)
            key_total = key_term if key_total is None else key_total + key_term
            value_total = value_term if value_total is None else value_total + value_term
        side[:, cols] = norm_backward(key_full[:, cols], 1.0, key_total).astype(BF16)
        shifted = slice((heads + head) * HEAD, (heads + head + 1) * HEAD)
        side[:, shifted] = value_total.astype(BF16)
    send[...] = dot_rt(query_grad[half:, :], wq[...]).astype(BF16)
    keep[...] = dot_rt(query_grad[:half, :], wq[...]).astype(BF16)


def patch_grad_kernel(code_list, group, side, wk, wv, keep, send):
    rows = side.shape[0] // len(code_list)
    cols = wk.shape[1]
    parts = []
    for code in code_list:
        start = pl.multiple_of((group[0] ^ code) * rows, rows)
        parts.append(side[pl.ds(start, rows), :])
    ordered = jnp.concatenate(parts, axis=0)
    total = dot_rt(ordered[:, :cols], wk[...]) + dot_rt(ordered[:, cols:], wv[...])
    half = keep.shape[0]
    keep[...] = total[:half].astype(BF16)
    send[...] = total[half:].astype(BF16)


def input_grad_kernel(residual_grad, bytes_half, near, far, gain, out):
    rows = out.shape[0]
    total = near[:rows].astype(F32) + far[...].astype(F32)
    states = bytes_half[:rows].astype(F32)
    out[...] = (residual_grad[...] + norm_backward(states, gain[...], total)).astype(BF16)


def pick_kernel(code_list, rows, index, *refs):
    sources, out, turned = refs[:-2], refs[-2], refs[-1]
    low = 0
    for source in sources:
        high = low + source.shape[0]
        turned[:, low:high] = source[...].T
        low = high
    for position, code in enumerate(code_list):
        start = pl.multiple_of((index[0] ^ code) * rows, rows)
        out[position * rows : (position + 1) * rows, :] = turned[pl.ds(start, rows), :]


def pick_transposed(sources, index, count, code_list):
    width = sources[0].shape[1]
    rows = width // count
    total = sum(source.shape[0] for source in sources)
    if rows % 16:
        turned = jnp.concatenate(sources).T
        return jnp.concatenate(
            [
                lax.dynamic_slice_in_dim(turned, (index[0] ^ code) * rows, rows, 0)
                for code in code_list
            ]
        )
    return pl.pallas_call(
        functools.partial(pick_kernel, code_list, rows),
        out_shape=jax.ShapeDtypeStruct((rows * len(code_list), total), BF16),
        in_specs=[pl.BlockSpec(memory_space=pltpu.SMEM)]
        + [pl.BlockSpec(memory_space=pltpu.VMEM)] * len(sources),
        out_specs=pl.BlockSpec(memory_space=pltpu.VMEM),
        scratch_shapes=[pltpu.VMEM((width, total), BF16)],
        compiler_params=room([], sources, 4 * width * total),
        name="pick",
    )(index, *sources)


def weight_grad_kernel(left, *refs):
    rights, (keep, send) = refs[:-2], refs[-2:]
    half = keep.shape[0]
    for out, rows in ((send, slice(half, None)), (keep, slice(0, half))):
        total, low = None, 0
        for right in rights:
            high = low + right.shape[0]
            term = dot(left[rows, low:high], right[...])
            total = term if total is None else total + term
            low = high
        out[...] = total.astype(BF16)


def weight_grad(left, rights):
    half = ((left.shape[0] // 2, rights[0].shape[1]), BF16)
    return vmem_call(weight_grad_kernel, [half, half], left, *rights, name="weight_grad")


def adam_kernel(scale, layout, spans, *refs):
    count = len(layout)
    terms = []
    taken = 0
    for width in spans:
        terms.append(refs[taken : taken + width])
        taken += width
    first_hbm, second_hbm = refs[taken : taken + 2]
    new_first_hbm, new_second_hbm, step_hbm = refs[-13:-10]
    first, second, new_first, new_second, step_out = refs[-10:-5]
    sems = refs[-5:]
    start = layout[0][0]
    total = sum(rows * cols for _, rows, cols, _ in layout)
    window = pl.ds(start, total)
    load_first = pltpu.make_async_copy(first_hbm.at[window], first, sems[0])
    load_second = pltpu.make_async_copy(second_hbm.at[window], second, sems[1])
    load_first.start()
    load_second.start()
    load_first.wait()
    load_second.wait()
    for refs_here, (offset, rows, cols, pick) in zip(terms, layout):
        for col in range(cols):
            at = pl.ds(offset - start + col, rows, stride=cols)
            grad = None
            for ref in refs_here:
                term = pick(ref, col).astype(F32)
                grad = term if grad is None else grad + term
            grad = grad * scale
            moment = beta_first * first[at, :] + (1.0 - beta_first) * grad
            square = beta_second * second[at, :] + (1.0 - beta_second) * grad * grad
            new_first[at, :] = moment
            new_second[at, :] = square
            step_out[at, :] = (
                moment / bias_first / (jnp.sqrt(square / bias_second) + adam_epsilon)
            )
    stores = [
        pltpu.make_async_copy(src, dst.at[window], sem)
        for src, dst, sem in zip(
            (new_first, new_second, step_out), (new_first_hbm, new_second_hbm, step_hbm), sems[2:]
        )
    ]
    for store in stores:
        store.start()
    for store in stores:
        store.wait()


def natural(ref, col):
    return ref[:, col * LANES : (col + 1) * LANES]


def adam_part(parts, start, first, second, previous, scale):
    layout, arrays, spans = [], [], []
    offset = start
    for terms, rows, cols, pick in parts:
        layout.append((offset, rows, cols, pick))
        arrays += terms
        spans.append(len(terms))
        offset += rows * cols
    count = len(arrays)
    total = offset - start
    shape = jax.ShapeDtypeStruct(first.shape, F32)
    hbm = pl.BlockSpec(memory_space=pl.ANY)
    vmem = pl.BlockSpec(memory_space=pltpu.VMEM)
    previous = () if previous is None else previous
    aliases = {count + 2 + k: k for k in range(len(previous))}
    outs = pl.pallas_call(
        functools.partial(adam_kernel, scale, tuple(layout), tuple(spans)),
        out_shape=(shape,) * 3,
        in_specs=[vmem] * count + [hbm] * (2 + len(previous)),
        out_specs=(hbm,) * 3,
        scratch_shapes=[pltpu.VMEM((total, LANES), F32)] * 5 + [pltpu.SemaphoreType.DMA] * 5,
        input_output_aliases=aliases,
        compiler_params=room([], arrays, 5 * 4 * LANES * total),
        name="adam",
    )(*arrays, first, second, *previous)
    return outs, offset


def pair_grad_kernel(normed_t, query_grad, attended_t, own, other, keep, send, count):
    rows_q = normed_t.shape[0] // count
    rows_o = attended_t.shape[0] // count
    width = keep.shape[1]
    half = own.shape[0]
    query_all = dot(normed_t[...], query_grad[...]).astype(BF16)
    output_all = (
        dot(attended_t[:, :half], own[...]) + dot(attended_t[:, half:], other[...])
    ).astype(BF16)
    rows = rows_q + own.shape[1] // width * rows_o
    for position in range(count):
        out = keep if position < count // 2 else send
        low = position % (count // 2) * rows
        out[low : low + rows_q, :] = query_all[position * rows_q : (position + 1) * rows_q]
        low += rows_q
        for piece in range(own.shape[1] // width):
            out[low : low + rows_o, :] = output_all[
                position * rows_o : (position + 1) * rows_o, piece * width : (piece + 1) * width
            ]
            low += rows_o


def shards(
    byte_states,
    patch_states,
    patch_lengths,
    cotangent,
    attention_gain,
    feedforward_gain,
    query_weight,
    key_weight,
    value_weight,
    output_weight,
    gate_weight,
    up_weight,
    down_weight,
    adam_first,
    adam_second,
):
    row_count, model = byte_states.shape
    n_dp = lax.axis_size("dp")
    n_heads = lax.axis_size("heads")
    dp = lax.axis_index("dp").astype(jnp.int32)
    dp_index = dp.reshape(1)
    group = lax.axis_index("heads").astype(jnp.int32).reshape(1)
    head_cols = query_weight.shape[1]
    heads = head_cols // HEAD
    hidden_here = gate_weight.shape[1]
    block = row_count // n_heads
    half = row_count // 2
    bits = [1 << k for k in range(n_dp.bit_length() - 1)]
    pair, rest = bits[0], bits[1:]
    head_codes = codes([1, 2])
    attention_row = attention_gain.reshape(1, -1)
    feedforward_row = feedforward_gain.reshape(1, -1)

    part_shape = ((half, model), BF16)
    (
        bytes_half, normed_bytes, query_full, key_full, value, query_n, key_n, probs, attended,
        keep, send,
    ) = vmem_call(
        functools.partial(attention_kernel, head_codes, heads),
        [
            part_shape,
            ((row_count, model), BF16),
            ((row_count, head_cols), F32),
            ((PATCHES, head_cols), F32),
            ((PATCHES, head_cols), BF16),
            ((row_count, head_cols), BF16),
            ((PATCHES, head_cols), BF16),
            ((heads, row_count, PATCHES), F32),
            ((row_count, head_cols), BF16),
            part_shape,
            part_shape,
        ],
        group, byte_states, patch_states, patch_lengths, attention_row,
        query_weight, key_weight, value_weight, output_weight,
        name="attention", smem=1,
    )
    near = add(keep, swap(send, "heads", 1))
    far = swap(near, "heads", 2)

    cot = rows_in_order(cotangent, group, head_codes, near)
    cot_own, cot_other = cot[:half], cot[half:]
    cot_pair_own = swap(cot_own, "dp", pair)
    hidden_grad = dot_rt(cot, down_weight)

    residual, normed_own = vmem_call(
        residual_kernel,
        [((half, model), F32), part_shape],
        bytes_half, near, far, feedforward_row,
        name="residual",
    )
    normed_other = swap(normed_own, "heads", 1)
    normed_pair_own = swap(normed_own, "dp", pair)
    gate_own, up_own, hidden_own, part_own = feedforward(
        normed_own, hidden_grad[:half], gate_weight, up_weight, True
    )
    gate_other, up_other, hidden_other, part_other = feedforward(
        normed_other, hidden_grad[half:], gate_weight, up_weight, True
    )
    near = add(part_own, swap(part_other, "heads", 1))
    far = swap(near, "heads", 2)

    cot_pair_other = swap(cot_pair_own, "heads", 1)
    cot_pair = jnp.concatenate([cot_pair_own, cot_pair_other])
    hidden_grad_pair = dot_rt(cot_pair, down_weight)
    normed_pair_other = swap(normed_pair_own, "heads", 1)
    normed_pair = jnp.concatenate([normed_pair_own, normed_pair_other])
    gate_pair, up_pair, hidden_pair = feedforward(
        normed_pair, hidden_grad_pair, gate_weight, up_weight, False
    )
    rest_codes = codes(rest)
    normed_t = pick_transposed(
        [normed_own, normed_other, normed_pair], dp_index, n_dp, rest_codes
    )
    hidden_t = pick_transposed(
        [hidden_own, hidden_other, hidden_pair], dp_index, n_dp, rest_codes
    )
    gate_terms = scatter_rest(*weight_grad(normed_t, [gate_own, gate_other, gate_pair]), rest)
    up_terms = scatter_rest(*weight_grad(normed_t, [up_own, up_other, up_pair]), rest)
    down_terms = scatter_rest(*weight_grad(hidden_t, [cot, cot_pair]), rest)

    residual_grad, own = vmem_call(
        residual_grad_kernel,
        [((block, model), F32), part_shape],
        residual, cot_own, near, far, feedforward_row,
        name="residual_grad",
    )
    other = swap(own, "heads", 1)

    query_grad, side, keep, send = vmem_call(
        functools.partial(attention_grad_kernel, heads),
        [
            ((row_count, head_cols), BF16),
            ((PATCHES, 2 * head_cols), BF16),
            part_shape,
            part_shape,
        ],
        own, other, output_weight, value, key_n, query_n, probs, query_full, key_full,
        query_weight,
        name="attention_grad",
    )
    near = add(keep, swap(send, "heads", 1))
    far = swap(near[block:], "heads", 2)
    patch_half = ((PATCHES // 2, patch_states.shape[1]), BF16)
    keep, send = vmem_call(
        functools.partial(patch_grad_kernel, head_codes),
        [patch_half, patch_half],
        group, side, key_weight, value_weight,
        name="patch_grad", smem=1,
    )
    patch_near, patch_send = add_halves(keep, swap(send, "heads", 1))
    patch_grad = add(patch_near, swap(patch_send, "heads", 2))
    (input_grad,) = vmem_call(
        input_grad_kernel,
        [((block, model), BF16)],
        residual_grad, bytes_half, near, far, attention_row,
        name="input_grad",
    )

    patch_order = codes(rest[::-1] + [pair])
    gathered = side
    for bit in rest[::-1] + [pair]:
        gathered = jnp.concatenate([gathered, swap(gathered, "dp", bit)])
    width = patch_states.shape[1] // n_dp
    columns = jnp.stack(
        [
            lax.dynamic_slice_in_dim(patch_states, (dp ^ code) * width, width, 1)
            for code in codes(bits)
        ]
    )
    for step in range(len(bits)):
        columns = columns.reshape(1 << step, -1, PATCHES, width) if step else columns[None]
        split = columns.shape[1] // 2
        received = swap(columns[:, split:], "dp", bits[step])
        columns = jnp.concatenate([columns[:, :split], received], axis=0)
    columns = columns.reshape(-1, width)
    gather_codes = [0]
    for bit in rest[::-1] + [pair]:
        gather_codes = gather_codes + [code | bit for code in gather_codes]
    column_codes = [0]
    for bit in bits:
        column_codes = column_codes + [code | bit for code in column_codes]
    places = [gather_codes.index(code) for code in column_codes]
    gathered = jnp.concatenate(
        [gathered[place * PATCHES : (place + 1) * PATCHES] for place in places]
    )
    patch_piece = dot_lt(columns, gathered)

    pair_codes = codes(bits)
    normed_bytes_t = pick_transposed([normed_bytes], dp_index, n_dp, pair_codes)
    attended_t = pick_transposed([attended], dp_index, n_dp, pair_codes)
    rows_q, rows_o = model // n_dp, head_cols // n_dp
    rows_both = rows_q + model // head_cols * rows_o
    chain = ((rows_both * n_dp // 2, head_cols), BF16)
    keep, send = vmem_call(
        functools.partial(pair_grad_kernel, count=n_dp),
        [chain, chain],
        normed_bytes_t, query_grad, attended_t, own, other,
        name="pair_grad",
    )
    pair_terms = list(scatter_rest(keep, send, bits))

    def query_at(ref, col):
        return ref[:rows_q, col * LANES : (col + 1) * LANES]

    def output_at(ref, col):
        per = head_cols // LANES
        low = rows_q + col // per * rows_o
        return ref[low : low + rows_o, col % per * LANES : (col % per + 1) * LANES]

    def key_at(ref, col):
        return ref[:, col * LANES : (col + 1) * LANES]

    def value_at(ref, col):
        return ref[:, head_cols + col * LANES : head_cols + (col + 1) * LANES]

    scale = float(row_count * n_dp) ** (-0.5)
    first = adam_first.reshape(-1, LANES)
    second = adam_second.reshape(-1, LANES)
    per = head_cols // LANES
    outs, at = adam_part(
        [
            (pair_terms, rows_q, per, query_at),
            ([patch_piece], width, per, key_at),
            ([patch_piece], width, per, value_at),
            (pair_terms, rows_o, model // LANES, output_at),
        ],
        0, first, second, None, scale,
    )
    for terms, cols in ((gate_terms, hidden_here), (up_terms, hidden_here), (down_terms, model)):
        rows = terms[0].shape[0]
        outs, at = adam_part(
            [(list(terms), rows, cols // LANES, natural)], at, first, second, outs, scale
        )
    outs = tuple(out.reshape(1, -1) for out in outs)
    return (input_grad, patch_grad) + outs


def solution(mesh):
    placed = (
        P("dp", None),
        P("dp", None),
        P("dp", None),
        P("dp", None),
        P(),
        P(),
        P(None, "heads"),
        P(None, "heads"),
        P(None, "heads"),
        P("heads", None),
        P(None, "heads"),
        P(None, "heads"),
        P("heads", None),
        P("heads", "dp"),
        P("heads", "dp"),
    )
    return jax.shard_map(
        shards,
        mesh=mesh,
        in_specs=placed,
        out_specs=(
            P(("dp", "heads"), None),
            P(("dp", "heads"), None),
            P("heads", "dp"),
            P("heads", "dp"),
            P("heads", "dp"),
        ),
        check_vma=False,
    )
```
